256 devices in a mesh: bead: 16 (over y, z_hi, core), bulk: 16 (over z_lo, x).
Axes of the slice: x: 4, y: 4, z: 8 (z_hi: 2, z_lo: 4; z = z_hi * 4 + z_lo), core: 2. Of those that a mesh axis runs over, the one named last changes fastest.
Arguments:
- coords: float32 [32, 3, 32768], P('bead', None, 'bulk'), may hold values from -0.08 to 16.08
- charges: float32 [32768], P('bulk'), may hold values from -0.07432544 to 0.07432544
- stiffness: float32 [32768], P('bulk'), may hold values from 2 to 20
- counts: int32 [16], P('bulk'), may hold values from 1024 to 2048, as said below
- contraction: float32 [2, 32], replicated, may hold values from 0 to 0.0625
- wavevectors: int32 [3, 10240], replicated, may hold values from -12 to 12, as said below
Outputs:
- bead_forces: float32 [32, 3, 32768], P('bead', None, 'bulk')
The draws below stay inside these ranges and needn't reach their ends.
Inputs may be any that keep to these rules, and one draw needn't show every extreme that they name: `counts`: slots of a domain at or past its count are padding; some domain is full. `wavevectors`: every column is a nonzero integer vector.
All inputs are finite; a program needn't handle non-finite values.
Results may differ from the reference program's by a relative error of at most 0.0003.
Values sent between devices are 32-bit elements; how exact they have to be, the bound alone decides.
No kernel may reach another device: no remote copies, remote signals or barrier semaphores. Data moves between devices by JAX's collectives and lax.ppermute only.
A program may use at most 64 MiB of HBM per device.

```python
import math
import jax
import jax.numpy as jnp
from jax import lax

BEADS = 32
REPLICAS = 2
K = 10240
KMAX = 12
ATOM_DEV = 128
SLOTS = 2048
DOMAINS = 16
ATOMS = 32768


def draw_coords(key, part):
    subkeys = jax.random.split(jax.random.fold_in(key, 11), 2)
    atom_index = jnp.arange(ATOMS, dtype=jnp.int32)
    domain = (atom_index // SLOTS).astype(jnp.float32)
    inside = jax.random.uniform(subkeys[0], (3, ATOMS), jnp.float32)
    centre = inside + jnp.stack([domain, jnp.zeros_like(domain), jnp.zeros_like(domain)])
    offsets = 0.02 * jnp.clip(jax.random.normal(subkeys[1], (BEADS, 3, ATOMS), jnp.float32), -4.0, 4.0)
    return centre[None, :, :] + offsets


def draw_counts(key, part):
    subkeys = jax.random.split(jax.random.fold_in(key, 23), 2)
    base = jax.random.randint(subkeys[0], (DOMAINS,), SLOTS // 2, SLOTS + 1)
    filled = jax.random.randint(subkeys[1], (), 0, DOMAINS)
    return jnp.where(jnp.arange(DOMAINS) == filled, SLOTS, base).astype(jnp.int32)


def draw_wavevectors(key, part):
    values = jax.random.randint(jax.random.fold_in(key, 37), (3, K), -KMAX, KMAX + 1)
    empty = jnp.all(values == 0, axis=0)
    third = jnp.where(empty, 1, values[2])
    return jnp.stack([values[0], values[1], third]).astype(jnp.int32)


def level_of(rng, extent, cuts, low, top_value):
    loudness = 1.0
    for dim, shards_of in cuts:
        heights = jax.random.uniform(jax.random.fold_in(jax.random.fold_in(rng, 6), dim), (shards_of,), jnp.float32, low / len(cuts), top_value / len(cuts))
        loudness = loudness * jnp.repeat(jnp.exp(heights), extent[dim] // shards_of).reshape((-1,) + (1,) * (len(extent) - 1 - dim))
    return loudness


def setup_inputs(seed: int = 0) -> dict:
    seeds = jax.random.split(jax.random.key(seed), 7)
    coords = draw_coords(jax.random.fold_in(seeds[6], 71), 0)
    charges = jnp.clip(jax.random.uniform(seeds[1], (ATOMS,), jnp.float32, -0.07432544, 0.07432544) * level_of(seeds[1], (ATOMS,), ((0, 16),), -0.4, 0.0), -0.07432544, 0.07432544)
    stiffness = jnp.clip(jnp.exp(math.log(20.0) - 2.3025851 * jax.random.uniform(seeds[2], (ATOMS,), jnp.float32) ** level_of(seeds[2], (ATOMS,), ((0, 16),), -0.2, 0.2)), 2.0, 20.0)
    counts = draw_counts(jax.random.fold_in(seeds[6], 71), 0)
    contraction = jnp.clip(jax.random.uniform(seeds[4], (REPLICAS, BEADS), jnp.float32, 0.0, 0.0625), 0.0, 0.0625)
    wavevectors = draw_wavevectors(jax.random.fold_in(seeds[6], 71), 0)
    return {"coords": coords, "charges": charges, "stiffness": stiffness, "counts": counts, "contraction": contraction, "wavevectors": wavevectors}


highest = lax.Precision.HIGHEST
alpha_split = 30.0


def wave_table(wavevectors, length_x):
    lengths = jnp.array([length_x, 1.0, 1.0], jnp.float32)
    wavenums = (2.0 * math.pi) * wavevectors.astype(jnp.float32) / lengths[:, None]
    ksquare = jnp.sum(wavenums * wavenums, axis=0)
    weight = (4.0 * math.pi / length_x) * jnp.exp(-ksquare / (4.0 * alpha_split * alpha_split)) / ksquare
    return wavenums, weight


def phase_table(wavenums, place):
    first = wavenums[0][:, None] * place[0][None, :] + wavenums[1][:, None] * place[1][None, :]
    return first + wavenums[2][:, None] * place[2][None, :]


def reference(coords, charges, stiffness, counts, contraction, wavevectors):
    wavenums, weight = wave_table(wavevectors, float(DOMAINS))
    atom_index = jnp.arange(ATOMS, dtype=jnp.int32)
    live = (atom_index % SLOTS) < counts[atom_index // SLOTS]
    charge = jnp.where(live, charges, 0.0)
    position = jnp.einsum("rp,pca->rca", contraction, coords, precision=highest)
    block_count = ATOMS // ATOM_DEV
    charge_blocks = charge.reshape(block_count, ATOM_DEV)
    results = []
    for replica in range(REPLICAS):
        place_blocks = position[replica].reshape(3, block_count, ATOM_DEV).transpose(1, 0, 2)

        def add_block(totals, inputs):
            place, charge_block = inputs
            phases = phase_table(wavenums, place)
            terms = jnp.stack([jnp.dot(jnp.cos(phases), charge_block, precision=highest),
                               jnp.dot(jnp.sin(phases), charge_block, precision=highest)])
            return totals + terms, None

        totals, _ = lax.scan(add_block, jnp.zeros((2, K), jnp.float32), (place_blocks, charge_blocks))

        def block_force(inputs):
            place, charge_block = inputs
            phases = phase_table(wavenums, place)
            mixture = (weight * totals[1])[:, None] * jnp.cos(phases) - (weight * totals[0])[:, None] * jnp.sin(phases)
            return -2.0 * charge_block[None, :] * jnp.dot(wavenums, mixture, precision=highest)

        pieces = lax.map(block_force, (place_blocks, charge_blocks))
        results.append(pieces.transpose(1, 0, 2).reshape(3, ATOMS))
    ewald_force = jnp.stack(results)
    spring = stiffness[None, None, :] * ((jnp.roll(coords, -1, 0) + jnp.roll(coords, 1, 0)) - 2.0 * coords)
    summed = jnp.einsum("rp,rca->pca", contraction, ewald_force, precision=highest) + spring
    return jnp.where(live[None, None, :], summed, 0.0)
```

```python
import math

import jax
import jax.numpy as jnp
import numpy as np
from jax import lax
from jax.experimental import pallas as pl
from jax.experimental.pallas import tpu as pltpu
from jax.sharding import PartitionSpec as P

alpha_split = 30.0
KDIM = 14
ROWS = KDIM * 8
TWO_PI = 2.0 * math.pi


def fitted(function, count):
    nodes = 0.125 + 0.125 * np.cos(np.pi * (np.arange(64) + 0.5) / 64)
    basis = np.polynomial.chebyshev.Chebyshev.fit(nodes, function(np.sqrt(nodes)), count - 1, domain=[0, 0.25])
    return [float(value) for value in basis.convert(kind=np.polynomial.Polynomial).coef]


COS_FIT = fitted(lambda u: np.cos(2 * np.pi * u), 9)
SIN_FIT = fitted(lambda u: np.sin(2 * np.pi * u) / u, 8)


def horner(coefficients, w):
    value = jnp.full_like(w, coefficients[-1])
    for coefficient in coefficients[-2::-1]:
        value = value * w + coefficient
    return value


def turn(cycles):
    u = cycles - jnp.round(cycles)
    w = u * u
    return horner(COS_FIT, w), u * horner(SIN_FIT, w)


def row_iota(rows, lanes, dim=0):
    return lax.broadcasted_iota(jnp.int32, (rows, lanes), dim)


def harmonics(fraction, start):
    order = (row_iota(8, fraction.shape[1]) + start).astype(jnp.float32)
    return turn(order * fraction)


def upper(c, s):
    c4, s4 = c[4:5], s[4:5]
    c8, s8 = c4 * c4 - s4 * s4, 2.0 * s4 * c4
    return c8 * c - s8 * s, s8 * c + c8 * s


def reduced(value):
    return value - jnp.round(value)


def split(value):
    high = value.astype(jnp.bfloat16)
    low = (value - high.astype(jnp.float32)).astype(jnp.bfloat16)
    return high, low


def tables(place, tabx, taby, replica, core, lanes):
    base = 3 * replica
    x = reduced(place[base : base + 1] * (1.0 / 16.0))
    y = reduced(place[base + 1 : base + 2])
    z = reduced(place[base + 2 : base + 3])
    cx, sx = harmonics(x, 8 * core)
    tabx[0:8, lanes] = cx
    tabx[8:16, lanes] = sx
    cy, sy = harmonics(y, 0)
    uy, vy = upper(cy, sy)
    taby[0:8, lanes] = cy
    taby[8:16, lanes] = uy
    taby[16:24, lanes] = sy
    taby[24:32, lanes] = vy
    cz, sz = harmonics(z, 0)
    uz, vz = upper(cz, sz)
    return jnp.concatenate([cz, uz], 0), jnp.concatenate([sz, vz], 0)


def partial_kernel(bead_ref, contraction_ref, coords_ref, out_ref):
    first = 2 * bead_ref[0]
    x0, x1 = coords_ref[0], coords_ref[1]
    out_ref[0:3, :] = contraction_ref[0, first] * x0 + contraction_ref[0, first + 1] * x1
    out_ref[3:6, :] = contraction_ref[1, first] * x0 + contraction_ref[1, first + 1] * x1
    out_ref[6:8, :] = jnp.zeros((2, x0.shape[1]), jnp.float32)


def histogram_kernel(bead_ref, wave_ref, out_ref, acc_ref):
    core = bead_ref[0] % 2
    step = 1024
    count = wave_ref.shape[1]
    acc_ref[...] = jnp.zeros_like(acc_ref)

    def body(index, carry):
        lanes = pl.ds(pl.multiple_of(index * step, step), step)
        h, k, l = wave_ref[0:1, lanes], wave_ref[1:2, lanes], wave_ref[2:3, lanes]
        flip = jnp.where(h < 0, -1, 1)
        h, k, l = h * flip, k * flip, l * flip
        s2 = jnp.where(k < 0, -1.0, 1.0)
        s3 = jnp.where(l < 0, -1.0, 1.0)
        k, l = jnp.abs(k), jnp.abs(l)
        hit = (h - 8 * core) == row_iota(8, step)
        blocks = []
        for sign in (jnp.ones_like(s2), s2, s3, s2 * s3):
            rows = jnp.where(hit, sign, 0.0)
            for order in range(KDIM):
                blocks.append(jnp.where(k == order, rows, 0.0))
        left = jnp.concatenate(blocks, 0).astype(jnp.bfloat16)
        lane = row_iota(128, step)
        right = jnp.where((l == (lane & 15)) & (lane < 32), 1.0, 0.0).astype(jnp.bfloat16)
        acc_ref[...] += lax.dot_general(
            left, right, (((1,), (1,)), ((), ())), preferred_element_type=jnp.float32
        )
        return carry

    lax.fori_loop(0, count // step, body, 0)
    row = row_iota(ROWS, 128)
    lane = row_iota(ROWS, 128, 1)
    kh = (TWO_PI / 16.0) * ((row & 7) + 8 * core).astype(jnp.float32)
    kk = TWO_PI * (row >> 3).astype(jnp.float32)
    kl = TWO_PI * (lane & 15).astype(jnp.float32)
    ksq = kh * kh + kk * kk + kl * kl
    safe = jnp.where(ksq > 0.0, ksq, 1.0)
    weight = (-2.0 * 4.0 * math.pi / 16.0) * jnp.exp(-safe / (4.0 * alpha_split * alpha_split)) / safe
    weight = jnp.where((lane < 32) & (ksq > 0.0), weight, 0.0)
    signed = jnp.where(lane < 16, weight, -weight)
    for moment in range(4):
        rows = slice(moment * ROWS, (moment + 1) * ROWS)
        out_ref[rows, :] = acc_ref[rows, :] * (weight if moment < 2 else signed)


def factor_kernel(bead_ref, counts_ref, near_ref, far_ref, charge_ref, out_ref, tabx, taby, right):
    core = bead_ref[0] % 2
    slots = near_ref.shape[1]
    step = 256
    right[64:128, :] = jnp.zeros((64, step), jnp.bfloat16)
    lane128 = row_iota(ROWS, 128, 1)
    for replica in range(2):

        def body(index, total, replica=replica):
            lanes = pl.ds(pl.multiple_of(index * step, step), step)
            place = near_ref[:, lanes] + far_ref[:, lanes]
            live = row_iota(1, step, 1) + index * step < counts_ref[0]
            charge = jnp.where(live, charge_ref[0:1, lanes], 0.0)
            cz, sz = tables(place, tabx, taby, replica, core, slice(None))
            high, low = split(jnp.concatenate([cz, sz], 0) * charge)
            right[0:32, :] = high
            right[32:64, :] = low
            blocks = []
            for beta in range(2):
                for alpha in range(2):
                    column = tabx[8 * alpha : 8 * alpha + 8, :]
                    for order in range(KDIM):
                        row = 16 * beta + order
                        blocks.append(column * taby[row : row + 1, :])
            high, low = split(jnp.concatenate(blocks, 0))
            other = right[...]
            dims = (((1,), (1,)), ((), ()))
            total = total + lax.dot_general(high, other, dims, preferred_element_type=jnp.float32)
            return total + lax.dot_general(low, other, dims, preferred_element_type=jnp.float32)

        total = lax.fori_loop(0, slots // step, body, jnp.zeros((4 * ROWS, 128), jnp.float32))
        packed = jnp.zeros((ROWS, 128), jnp.float32)
        for group in range(4):
            part = total[group * ROWS : (group + 1) * ROWS]
            part = part + pltpu.roll(part, 96, 1)
            part = jnp.where(lane128 < 32, part, 0.0)
            packed = packed + (pltpu.roll(part, 32 * group, 1) if group else part)
        out_ref[replica * ROWS : (replica + 1) * ROWS, :] = packed


def force_kernel(
    bead_ref, counts_ref, near_ref, far_ref, charge_ref, s0_ref, s1_ref, s2_ref, s3_ref, w_ref,
    out_ref, tabx, taby, basis, slope, mixed,
):
    core = bead_ref[0] % 2
    slots = near_ref.shape[1]
    step = 256
    lane128 = row_iota(ROWS, 128, 1)
    w0, w2 = w_ref[0:ROWS, :], w_ref[ROWS : 2 * ROWS, :]
    w3, w23 = w_ref[2 * ROWS : 3 * ROWS, :], w_ref[3 * ROWS : 4 * ROWS, :]
    order16 = TWO_PI * row_iota(16, step).astype(jnp.float32)
    kx = (TWO_PI / 16.0) * (row_iota(8, step) + 8 * core).astype(jnp.float32)
    for replica in range(2):
        rows = slice(replica * ROWS, (replica + 1) * ROWS)
        total = (s0_ref[rows, :] + s1_ref[rows, :]) + (s2_ref[rows, :] + s3_ref[rows, :])
        quads = [total if group == 0 else pltpu.roll(total, 128 - 32 * group, 1) for group in range(4)]
        swapped = [
            jnp.where(lane128 < 16, pltpu.roll(quad, 112, 1), pltpu.roll(quad, 16, 1)) for quad in quads
        ]
        cc, sc, cs, ss = quads
        tcc, tsc, tcs, tss = swapped
        results = (
            w0 * cc - w2 * ss - w3 * tsc - w23 * tcs,
            w0 * sc + w2 * cs + w3 * tcc - w23 * tss,
            w0 * cs + w2 * sc - w3 * tss + w23 * tcc,
            w0 * ss - w2 * cc + w3 * tcs + w23 * tsc,
        )
        for group, value in enumerate(results):
            high = value.astype(jnp.bfloat16).astype(jnp.float32)
            low = value - high
            spread = (high + pltpu.roll(high, 32, 1)) + (pltpu.roll(low, 64, 1) + pltpu.roll(low, 96, 1))
            mixed[group * ROWS : (group + 1) * ROWS, :] = spread.astype(jnp.bfloat16)

        def body(index, carry, replica=replica):
            lanes = pl.ds(pl.multiple_of(index * step, step), step)
            place = near_ref[:, lanes] + far_ref[:, lanes]
            live = row_iota(1, step, 1) + index * step < counts_ref[0]
            charge = jnp.where(live, charge_ref[0:1, lanes], 0.0)
            cz, sz = tables(place, tabx, taby, replica, core, slice(None))
            for target, value in (
                (basis, jnp.concatenate([cz, sz], 0)),
                (slope, jnp.concatenate([-order16 * sz, order16 * cz], 0)),
            ):
                high, low = split(value)
                target[0:32, :] = high
                target[32:64, :] = low
                target[64:96, :] = high
                target[96:128, :] = low
            flat = jnp.dot(mixed[...], basis[...], preferred_element_type=jnp.float32)
            tilt = jnp.dot(mixed[...], slope[...], preferred_element_type=jnp.float32)
            along, across, upward = [], [], []
            for alpha in range(2):
                one = two = three = jnp.zeros((8, step), jnp.float32)
                for order in range(KDIM):
                    c, s = taby[order : order + 1, :], taby[16 + order : 17 + order, :]
                    at = alpha * ROWS + 8 * order
                    ta, tb = flat[at : at + 8], flat[at + 2 * ROWS : at + 2 * ROWS + 8]
                    one = one + (c * ta + s * tb)
                    if order:
                        two = two + (TWO_PI * order) * (c * tb - s * ta)
                    three = three + (c * tilt[at : at + 8] + s * tilt[at + 2 * ROWS : at + 2 * ROWS + 8])
                along.append(one)
                across.append(two)
                upward.append(three)
            cx, sx = tabx[0:8, :], tabx[8:16, :]
            fx = jnp.sum(kx * (cx * along[1] - sx * along[0]), 0, keepdims=True)
            fy = jnp.sum(cx * across[0] + sx * across[1], 0, keepdims=True)
            fz = jnp.sum(cx * upward[0] + sx * upward[1], 0, keepdims=True)
            base = 3 * replica
            out_ref[base : base + 1, lanes] = fx * charge
            out_ref[base + 1 : base + 2, lanes] = fy * charge
            out_ref[base + 2 : base + 3, lanes] = fz * charge
            return carry

        lax.fori_loop(0, slots // step, body, 0)
    out_ref[6:8, :] = jnp.zeros((2, slots), jnp.float32)


def output_kernel(
    bead_ref, counts_ref, contraction_ref, near_ref, far_ref, coords_ref, low_ref, high_ref, stiff_ref, out_ref
):
    first = 2 * bead_ref[0]
    total = near_ref[...] + far_ref[...]
    f0, f1 = total[0:3], total[3:6]
    x0, x1 = coords_ref[0], coords_ref[1]
    stiff = stiff_ref[...]
    live = row_iota(1, x0.shape[1], 1) < counts_ref[0]
    for bead, (before, here, after) in enumerate(((low_ref[0], x0, x1), (x0, x1, high_ref[0]))):
        spring = stiff * ((after + before) - 2.0 * here)
        value = contraction_ref[0, first + bead] * f0 + contraction_ref[1, first + bead] * f1 + spring
        out_ref[bead] = jnp.where(live, value, 0.0)


def vmem():
    return pl.BlockSpec(memory_space=pltpu.VMEM)


def smem():
    return pl.BlockSpec(memory_space=pltpu.SMEM)


def call(kernel, shape, scalars, arrays, scratch, name, flops, limit=16 << 20):
    return pl.pallas_call(
        kernel,
        out_shape=jax.ShapeDtypeStruct(shape, jnp.float32),
        in_specs=[smem()] * len(scalars) + [vmem()] * len(arrays),
        out_specs=vmem(),
        scratch_shapes=scratch,
        name=name,
        compiler_params=pltpu.CompilerParams(vmem_limit_bytes=limit),
        cost_estimate=pl.CostEstimate(flops=flops, bytes_accessed=1 << 18, transcendentals=0),
    )(*scalars, *arrays)


def call_partial(bead, contraction, coords):
    return call(partial_kernel, (8, coords.shape[2]), (bead, contraction), (coords,), [], "partial", 1 << 16)


def call_histogram(bead, wavevectors):
    scratch = [pltpu.VMEM((4 * ROWS, 128), jnp.float32)]
    return call(histogram_kernel, (4 * ROWS, 128), (bead,), (wavevectors,), scratch, "histogram", 1 << 32)


def call_factor(bead, counts, near, far, charge):
    scratch = [
        pltpu.VMEM((16, 256), jnp.float32),
        pltpu.VMEM((32, 256), jnp.float32),
        pltpu.VMEM((128, 256), jnp.bfloat16),
    ]
    return call(factor_kernel, (2 * ROWS, 128), (bead, counts), (near, far, charge), scratch, "factor", 1 << 32)


def call_force(bead, counts, near, far, charge, sums, weights):
    scratch = [
        pltpu.VMEM((16, 256), jnp.float32),
        pltpu.VMEM((32, 256), jnp.float32),
        pltpu.VMEM((128, 256), jnp.bfloat16),
        pltpu.VMEM((128, 256), jnp.bfloat16),
        pltpu.VMEM((4 * ROWS, 128), jnp.bfloat16),
    ]
    return call(
        force_kernel, near.shape, (bead, counts), (near, far, charge, *sums, weights), scratch, "force", 1 << 32
    )


def call_output(bead, counts, contraction, near, far, coords, low, high, stiffness):
    return call(
        output_kernel, coords.shape, (bead, counts, contraction), (near, far, coords, low, high, stiffness), [],
        "output", 1 << 16,
    )


def shards(mesh_shape, coords, charges, stiffness, counts, contraction, wavevectors):
    beads, bulks = mesh_shape["bead"], mesh_shape["bulk"]
    bead = lax.axis_index("bead").astype(jnp.int32).reshape(1)
    ys, xs, zs = beads // 4, 4, 2 * (bulks // 4)

    def over_bead(value, target):
        return lax.ppermute(value, "bead", [(i, target(i)) for i in range(beads)])

    def over_x(value, distance):
        pairs = [(i, i // xs * xs + (i + distance) % xs) for i in range(bulks)]
        return lax.ppermute(value, "bulk", pairs)

    def over_z(value, distance):
        pairs = []
        for b in range(beads):
            for k in range(bulks):
                z = (b // 2 % 2) * (zs // 2) + k // xs
                z = (z + distance) % zs
                there = b - b // 2 % 2 * 2 + z // (zs // 2) * 2
                pairs.append((b * bulks + k, there * bulks + z % (zs // 2) * xs + k % xs))
        return lax.ppermute(value, ("bead", "bulk"), pairs)

    charge = charges.reshape(1, -1)
    stiff = stiffness.reshape(1, -1)
    weights = call_histogram(bead, wavevectors)
    part = call_partial(bead, contraction, coords)
    part = part + over_bead(part, lambda i: i ^ 1)
    moved = [over_bead(part, lambda i, d=d: (i + 4 * d) % (4 * ys)) for d in (1, 3, 2)]
    near = (part + moved[0]) + (moved[1] + moved[2])
    far = over_bead(near, lambda i: i ^ 2)
    sums = call_factor(bead, counts, near, far, charge)
    edge_low, edge_high, sums = lax.optimization_barrier((coords[1:2], coords[0:1], sums))
    low = over_bead(edge_low, lambda i: (i + 1) % beads)
    high = over_bead(edge_high, lambda i: (i - 1) % beads)
    moved = [over_x(sums, d) for d in (1, 3, 2)]
    sums = (sums + moved[0]) + (moved[1] + moved[2])
    parts = [sums] + [over_z(sums, d) for d in (1, 7, 2)]
    force = call_force(bead, counts, near, far, charge, parts, weights)
    other = over_bead(force, lambda i: i ^ 1)
    return call_output(bead, counts, contraction, force, other, coords, low, high, stiff)


def solution(mesh):
    shape = dict(mesh.shape)
    return jax.shard_map(
        lambda *arrays: shards(shape, *arrays),
        mesh=mesh,
        in_specs=(P("bead", None, "bulk"), P("bulk"), P("bulk"), P("bulk"), P(), P()),
        out_specs=P("bead", None, "bulk"),
        check_vma=False,
    )
```

```python
import math

import jax
import jax.numpy as jnp
import numpy as np
from jax import lax
from jax.experimental import pallas as pl
from jax.experimental.pallas import tpu as pltpu
from jax.sharding import PartitionSpec as P

alpha_split = 30.0
KDIM = 13
ROWS = KDIM * 16
STEP = 256
TWO_PI = 2.0 * math.pi


def fitted(function, count):
    nodes = 0.125 + 0.125 * np.cos(np.pi * (np.arange(64) + 0.5) / 64)
    basis = np.polynomial.chebyshev.Chebyshev.fit(nodes, function(np.sqrt(nodes)), count - 1, domain=[0, 0.25])
    return [float(value) for value in basis.convert(kind=np.polynomial.Polynomial).coef]


COS_FIT = fitted(lambda u: np.cos(2 * np.pi * u), 9)
SIN_FIT = fitted(lambda u: np.sin(2 * np.pi * u) / u, 8)


def horner(coefficients, w):
    value = jnp.full_like(w, coefficients[-1])
    for coefficient in coefficients[-2::-1]:
        value = value * w + coefficient
    return value


def turn(cycles):
    u = cycles - jnp.round(cycles)
    w = u * u
    return horner(COS_FIT, w), u * horner(SIN_FIT, w)


def row_iota(rows, lanes, dim=0):
    return lax.broadcasted_iota(jnp.int32, (rows, lanes), dim)


def harmonics(fraction, start):
    order = (row_iota(8, fraction.shape[1]) + start).astype(jnp.float32)
    return turn(order * fraction)


def upper(c, s):
    c4, s4 = c[4:5], s[4:5]
    c8, s8 = c4 * c4 - s4 * s4, 2.0 * s4 * c4
    return c8 * c - s8 * s, s8 * c + c8 * s


def reduced(value):
    return value - jnp.round(value)


def split(value):
    high = value.astype(jnp.bfloat16)
    low = (value - high.astype(jnp.float32)).astype(jnp.bfloat16)
    return high, low


def tables(place, tabx, taby):
    found = []
    for fraction in (
        reduced(place[0:1] * (1.0 / 16.0)),
        reduced(place[1:2]),
        reduced(place[2:3]),
    ):
        c, s = harmonics(fraction, 0)
        cu, su = upper(c, s)
        found.append((c, cu, s, su))
    for target, parts in ((tabx, found[0]), (taby, found[1])):
        for index, part in enumerate(parts):
            target[8 * index : 8 * index + 8, :] = part
    return jnp.concatenate(found[2][0:2], 0), jnp.concatenate(found[2][2:4], 0)


def partial_kernel(bead_ref, contraction_ref, coords_ref, keep_ref, send_ref):
    bead = bead_ref[0]
    core = bead % 2
    first = 2 * bead
    keep_ref[...] = jnp.zeros_like(keep_ref)
    send_ref[...] = jnp.zeros_like(send_ref)
    for c in range(3):
        x0, x1 = coords_ref[c, 0:1, :], coords_ref[c, 1:2, :]
        keep_ref[c : c + 1, :] = contraction_ref[core, first] * x0 + contraction_ref[core, first + 1] * x1
        send_ref[c : c + 1, :] = (
            contraction_ref[1 - core, first] * x0 + contraction_ref[1 - core, first + 1] * x1
        )
        send_ref[3 + c : 4 + c, :] = jnp.where(core == 0, x0, x1)
        send_ref[8 + c : 9 + c, :] = jnp.where(core == 0, x1, x0)


def histogram_kernel(wave_ref, out_ref, acc_ref):
    step = 1024
    count = wave_ref.shape[1]
    acc_ref[...] = jnp.zeros_like(acc_ref)

    def body(index, carry):
        lanes = pl.ds(pl.multiple_of(index * step, step), step)
        h, k, l = wave_ref[0:1, lanes], wave_ref[1:2, lanes], wave_ref[2:3, lanes]
        flip = jnp.where(h < 0, -1, 1)
        h, k, l = h * flip, k * flip, l * flip
        s2 = jnp.where(k < 0, -1.0, 1.0)
        s3 = jnp.where(l < 0, -1.0, 1.0)
        k, l = jnp.abs(k), jnp.abs(l)
        row = row_iota(16, step)
        hit = h == row
        left = [jnp.where(hit, sign, 0.0) for sign in (jnp.ones_like(s2), s2, s3, s2 * s3)]
        ones = jnp.where(l == row, 1.0, 0.0)
        right = [jnp.where(k == order, ones, 0.0) for order in range(KDIM)]
        acc_ref[:, 0:ROWS] += lax.dot_general(
            jnp.concatenate(left, 0).astype(jnp.bfloat16),
            jnp.concatenate(right, 0).astype(jnp.bfloat16),
            (((1,), (1,)), ((), ())),
            preferred_element_type=jnp.float32,
        )
        return carry

    lax.fori_loop(0, count // step, body, 0)
    lane = row_iota(16, 128, 1)
    kh = (TWO_PI / 16.0) * row_iota(16, 128).astype(jnp.float32)
    kl = TWO_PI * (lane & 15).astype(jnp.float32)
    for order in range(KDIM):
        ksq = kh * kh + (TWO_PI * order) ** 2 + kl * kl
        safe = jnp.where(ksq > 0.0, ksq, 1.0)
        weight = (-2.0 * 4.0 * math.pi / 16.0) * jnp.exp(-safe / (4.0 * alpha_split * alpha_split)) / safe
        weight = jnp.where((lane < 32) & (ksq > 0.0), weight, 0.0)
        signed = jnp.where(lane < 16, weight, -weight)
        tile = order // 8
        for moment in range(4):
            counts = acc_ref[16 * moment : 16 * moment + 16, 128 * tile : 128 * tile + 128]
            at = 16 * (order % 8)
            low = pltpu.roll(counts, 128 - at, 1) if at else counts
            both = jnp.where(lane < 16, low, pltpu.roll(low, 16, 1))
            rows = slice(moment * ROWS + 16 * order, moment * ROWS + 16 * order + 16)
            out_ref[rows, :] = both * (weight if moment < 2 else signed)


def factor_kernel(counts_ref, near_ref, far_ref, charge_ref, out_ref, tabx, taby, right, total_ref):
    slots = near_ref.shape[1]
    right[64:128, :] = jnp.zeros((64, STEP), jnp.bfloat16)
    total_ref[...] = jnp.zeros_like(total_ref)

    def body(index, carry):
        lanes = pl.ds(pl.multiple_of(index * STEP, STEP), STEP)
        place = near_ref[0:3, lanes] + far_ref[0:3, lanes]
        live = row_iota(1, STEP, 1) + index * STEP < counts_ref[0]
        charge = jnp.where(live, charge_ref[0:1, lanes], 0.0)
        cz, sz = tables(place, tabx, taby)
        high, low = split(jnp.concatenate([cz, sz], 0) * charge)
        right[0:32, :] = high
        right[32:64, :] = low
        other = right[...]
        dims = (((1,), (1,)), ((), ()))
        for beta in range(2):
            for alpha in range(2):
                column = tabx[16 * alpha : 16 * alpha + 16, :]
                blocks = [
                    column * taby[16 * beta + order : 16 * beta + order + 1, :] for order in range(KDIM)
                ]
                high, low = split(jnp.concatenate(blocks, 0))
                rows = slice((2 * beta + alpha) * ROWS, (2 * beta + alpha + 1) * ROWS)
                total_ref[rows, :] += lax.dot_general(
                    high, other, dims, preferred_element_type=jnp.float32
                ) + lax.dot_general(low, other, dims, preferred_element_type=jnp.float32)
        return carry

    lax.fori_loop(0, slots // STEP, body, 0)
    lane128 = row_iota(ROWS, 128, 1)
    packed = jnp.zeros((ROWS, 128), jnp.float32)
    for group in range(4):
        part = total_ref[group * ROWS : (group + 1) * ROWS, :]
        part = part + pltpu.roll(part, 96, 1)
        part = jnp.where(lane128 < 32, part, 0.0)
        packed = packed + (pltpu.roll(part, 32 * group, 1) if group else part)
    out_ref[...] = packed


def force_kernel(
    counts_ref, near_ref, far_ref, charge_ref, s0_ref, s1_ref, s2_ref, s3_ref, w_ref,
    out_ref, tabx, taby, basis, slope, mixed,
):
    slots = near_ref.shape[1]
    lane128 = row_iota(ROWS, 128, 1)
    w0, w2 = w_ref[0:ROWS, :], w_ref[ROWS : 2 * ROWS, :]
    w3, w23 = w_ref[2 * ROWS : 3 * ROWS, :], w_ref[3 * ROWS : 4 * ROWS, :]
    total = (s0_ref[...] + s1_ref[...]) + (s2_ref[...] + s3_ref[...])
    quads = [total if group == 0 else pltpu.roll(total, 128 - 32 * group, 1) for group in range(4)]
    swapped = [
        jnp.where(lane128 < 16, pltpu.roll(quad, 112, 1), pltpu.roll(quad, 16, 1)) for quad in quads
    ]
    cc, sc, cs, ss = quads
    tcc, tsc, tcs, tss = swapped
    results = (
        w0 * cc - w2 * ss - w3 * tsc - w23 * tcs,
        w0 * sc + w2 * cs + w3 * tcc - w23 * tss,
        w0 * cs + w2 * sc - w3 * tss + w23 * tcc,
        w0 * ss - w2 * cc + w3 * tcs + w23 * tsc,
    )
    for group, value in enumerate(results):
        high = value.astype(jnp.bfloat16).astype(jnp.float32)
        low = value - high
        spread = (high + pltpu.roll(high, 32, 1)) + (pltpu.roll(low, 64, 1) + pltpu.roll(low, 96, 1))
        mixed[group * ROWS : (group + 1) * ROWS, :] = spread.astype(jnp.bfloat16)
    order16 = TWO_PI * row_iota(16, STEP).astype(jnp.float32)
    kx = order16 * (1.0 / 16.0)

    def body(index, carry):
        lanes = pl.ds(pl.multiple_of(index * STEP, STEP), STEP)
        place = near_ref[0:3, lanes] + far_ref[0:3, lanes]
        live = row_iota(1, STEP, 1) + index * STEP < counts_ref[0]
        charge = jnp.where(live, charge_ref[0:1, lanes], 0.0)
        cz, sz = tables(place, tabx, taby)
        for target, value in (
            (basis, jnp.concatenate([cz, sz], 0)),
            (slope, jnp.concatenate([-order16 * sz, order16 * cz], 0)),
        ):
            high, low = split(value)
            target[0:32, :] = high
            target[32:64, :] = low
            target[64:96, :] = high
            target[96:128, :] = low
        along, across, upward = [], [], []
        for alpha in range(2):
            both = [mixed[(2 * beta + alpha) * ROWS : (2 * beta + alpha + 1) * ROWS, :] for beta in range(2)]
            flat = [jnp.dot(m, basis[...], preferred_element_type=jnp.float32) for m in both]
            tilt = [jnp.dot(m, slope[...], preferred_element_type=jnp.float32) for m in both]
            one = two = three = jnp.zeros((16, STEP), jnp.float32)
            for order in range(KDIM):
                c, s = taby[order : order + 1, :], taby[16 + order : 17 + order, :]
                rows = slice(16 * order, 16 * order + 16)
                one = one + (c * flat[0][rows] + s * flat[1][rows])
                if order:
                    two = two + (TWO_PI * order) * (c * flat[1][rows] - s * flat[0][rows])
                three = three + (c * tilt[0][rows] + s * tilt[1][rows])
            along.append(one)
            across.append(two)
            upward.append(three)
        cx, sx = tabx[0:16, :], tabx[16:32, :]
        fx = jnp.sum(kx * (cx * along[1] - sx * along[0]), 0, keepdims=True)
        fy = jnp.sum(cx * across[0] + sx * across[1], 0, keepdims=True)
        fz = jnp.sum(cx * upward[0] + sx * upward[1], 0, keepdims=True)
        out_ref[0:1, lanes] = fx * charge
        out_ref[1:2, lanes] = fy * charge
        out_ref[2:3, lanes] = fz * charge
        return carry

    lax.fori_loop(0, slots // STEP, body, 0)


def output_kernel(
    bead_ref, counts_ref, contraction_ref, own_ref, other_ref, coords_ref, inner_ref, far_ref, stiff_ref, out_ref
):
    bead = bead_ref[0]
    core = bead % 2
    first = 2 * bead
    stiff = stiff_ref[...]
    live = row_iota(1, stiff.shape[1], 1) < counts_ref[0]
    for c in range(3):
        own, other = own_ref[c : c + 1, :], other_ref[c : c + 1, :]
        x0, x1 = coords_ref[c, 0:1, :], coords_ref[c, 1:2, :]
        inner, outer = inner_ref[8 + c : 9 + c, :], far_ref[3 + c : 4 + c, :]
        low = jnp.where(core == 0, outer, inner)
        high = jnp.where(core == 0, inner, outer)
        for index, (before, here, after) in enumerate(((low, x0, x1), (x0, x1, high))):
            spring = stiff * ((after + before) - 2.0 * here)
            mine = contraction_ref[core, first + index] * own
            value = (mine + contraction_ref[1 - core, first + index] * other) + spring
            out_ref[c, index : index + 1, :] = jnp.where(live, value, 0.0)


def vmem():
    return pl.BlockSpec(memory_space=pltpu.VMEM)


def smem():
    return pl.BlockSpec(memory_space=pltpu.SMEM)


def call(kernel, shapes, scalars, arrays, scratch, name, flops, limit=16 << 20):
    outs = [jax.ShapeDtypeStruct(shape, jnp.float32) for shape in shapes]
    result = pl.pallas_call(
        kernel,
        out_shape=outs,
        in_specs=[smem()] * len(scalars) + [vmem()] * len(arrays),
        out_specs=[vmem()] * len(outs),
        scratch_shapes=scratch,
        name=name,
        compiler_params=pltpu.CompilerParams(vmem_limit_bytes=limit),
        cost_estimate=pl.CostEstimate(flops=flops, bytes_accessed=1 << 18, transcendentals=0),
    )(*scalars, *arrays)
    return result if len(outs) > 1 else result[0]


def call_partial(bead, contraction, coords):
    slots = coords.shape[2]
    return call(
        partial_kernel, [(8, slots), (16, slots)], (bead, contraction), (coords,), [], "partial", 1 << 16
    )


def call_histogram(wavevectors):
    scratch = [pltpu.VMEM((64, 256), jnp.float32)]
    return call(histogram_kernel, [(4 * ROWS, 128)], (), (wavevectors,), scratch, "histogram", 1 << 32)


def table_scratch():
    return [pltpu.VMEM((32, STEP), jnp.float32), pltpu.VMEM((32, STEP), jnp.float32)]


def call_factor(counts, near, far, charge):
    scratch = table_scratch() + [
        pltpu.VMEM((128, STEP), jnp.bfloat16),
        pltpu.VMEM((4 * ROWS, 128), jnp.float32),
    ]
    return call(factor_kernel, [(ROWS, 128)], (counts,), (near, far, charge), scratch, "factor", 1 << 32)


def call_force(counts, near, far, charge, sums, weights):
    scratch = table_scratch() + [
        pltpu.VMEM((128, STEP), jnp.bfloat16),
        pltpu.VMEM((128, STEP), jnp.bfloat16),
        pltpu.VMEM((4 * ROWS, 128), jnp.bfloat16),
    ]
    arrays = (near, far, charge, *sums, weights)
    return call(force_kernel, [(3, near.shape[1])], (counts,), arrays, scratch, "force", 1 << 32)


def call_output(bead, counts, contraction, own, other, coords, inner, far, stiffness):
    arrays = (own, other, coords, inner, far, stiffness)
    return call(
        output_kernel, [coords.shape], (bead, counts, contraction), arrays, [], "output", 1 << 16
    )


def shards(mesh_shape, coords, charges, stiffness, counts, contraction, wavevectors):
    beads, bulks = mesh_shape["bead"], mesh_shape["bulk"]
    ys, xs, zs = beads // 4, 4, 2 * (bulks // 4)
    index = lax.axis_index("bead").astype(jnp.int32)
    bead = index.reshape(1)
    core, z_hi = index % 2, index // 2 % 2

    def over_bead(value, target):
        return lax.ppermute(value, "bead", [(i, target(i)) for i in range(beads)])

    def over_x(value, distance):
        pairs = [(i, i // xs * xs + (i + distance) % xs) for i in range(bulks)]
        return lax.ppermute(value, "bulk", pairs)

    def over_z(value, distance):
        pairs = []
        for b in range(beads):
            for k in range(bulks):
                z = (b // 2 % 2) * (zs // 2) + k // xs
                z = (z + distance) % zs
                there = b - b // 2 % 2 * 2 + z // (zs // 2) * 2
                pairs.append((b * bulks + k, there * bulks + z % (zs // 2) * xs + k % xs))
        return lax.ppermute(value, ("bead", "bulk"), pairs)

    charge = charges.reshape(1, -1)
    stiff = stiffness.reshape(1, -1)
    coords = coords.transpose(1, 0, 2)
    weights = call_histogram(wavevectors)
    keep, send = call_partial(bead, contraction, coords)
    inner = over_bead(send, lambda i: i ^ 1)
    chip = keep + inner[0:8]
    before, after, across = [
        over_bead(chip, lambda i, d=d: (i + 4 * d) % (4 * ys)) for d in (1, ys - 1, 2)
    ]
    passing = jnp.where(core == 0, jnp.where(z_hi == 1, before, chip), jnp.where(z_hi == 0, after, chip))
    positions = lax.broadcasted_iota(jnp.int32, chip.shape, 0) < 3
    near = jnp.where(positions, (chip + before) + (after + across), passing)
    far = over_bead(near, lambda i: i ^ 2)
    sums = call_factor(counts, near, far, charge)
    moved = [over_x(sums, d) for d in (1, 3, 2)]
    sums = (sums + moved[0]) + (moved[1] + moved[2])
    parts = [sums] + [over_z(sums, d) for d in (1, zs - 1, 2)]
    force = call_force(counts, near, far, charge, parts, weights)
    other = over_bead(force, lambda i: i ^ 1)
    result = call_output(bead, counts, contraction, force, other, coords, inner, far, stiff)
    return result.transpose(1, 0, 2)


def solution(mesh):
    shape = dict(mesh.shape)
    return jax.shard_map(
        lambda *arrays: shards(shape, *arrays),
        mesh=mesh,
        in_specs=(P("bead", None, "bulk"), P("bulk"), P("bulk"), P("bulk"), P(), P()),
        out_specs=P("bead", None, "bulk"),
        check_vma=False,
    )
```

```python
import math

import jax
import jax.numpy as jnp
import numpy as np
from jax import lax
from jax.experimental import pallas as pl
from jax.experimental.pallas import tpu as pltpu
from jax.sharding import PartitionSpec as P

alpha_split = 30.0
KTOP = 12
SPAN = 2 * KTOP + 1
XROWS = 2 * KTOP
GROUPS = 5
STEP = 256
TWO_PI = 2.0 * math.pi


def fitted(function, count):
    nodes = 0.125 + 0.125 * np.cos(np.pi * (np.arange(64) + 0.5) / 64)
    basis = np.polynomial.chebyshev.Chebyshev.fit(nodes, function(np.sqrt(nodes)), count - 1, domain=[0, 0.25])
    return [float(value) for value in basis.convert(kind=np.polynomial.Polynomial).coef]


COS_FIT = fitted(lambda u: np.cos(2 * np.pi * u), 9)
SIN_FIT = fitted(lambda u: np.sin(2 * np.pi * u) / u, 8)


def horner(coefficients, w):
    value = jnp.full_like(w, coefficients[-1])
    for coefficient in coefficients[-2::-1]:
        value = value * w + coefficient
    return value


def turn(cycles):
    u = cycles - jnp.round(cycles)
    w = u * u
    return horner(COS_FIT, w), u * horner(SIN_FIT, w)


def row_iota(rows, lanes, dim=0):
    return lax.broadcasted_iota(jnp.int32, (rows, lanes), dim)


def harmonics(fraction, start):
    order = (row_iota(8, fraction.shape[1]) + start).astype(jnp.float32)
    return turn(order * fraction)


def upper(c, s):
    c4, s4 = c[4:5], s[4:5]
    c8, s8 = c4 * c4 - s4 * s4, 2.0 * s4 * c4
    return c8 * c - s8 * s, s8 * c + c8 * s


def reduced(value):
    return value - jnp.round(value)


def split(value):
    high = value.astype(jnp.bfloat16)
    low = (value - high.astype(jnp.float32)).astype(jnp.bfloat16)
    return high, low


def tables(place, tabx, taby, tabz, lanes):
    x = reduced(place[0:1] * (1.0 / 16.0))
    order = row_iota(8, x.shape[1]).astype(jnp.float32)
    c, s = turn((order + 1.0) * x)
    c8, s8 = c[7:8], s[7:8]
    early = row_iota(8, x.shape[1]) < 4
    low_c = jnp.where(early, c, pltpu.roll(c, 4, 0))
    low_s = jnp.where(early, s, pltpu.roll(s, 4, 0))
    tabx[0:8, lanes] = c
    tabx[8:16, lanes] = jnp.where(early, c8 * low_c - s8 * low_s, s8 * low_c + c8 * low_s)
    tabx[16:24, lanes] = s
    for target, fraction in ((taby, reduced(place[1:2])), (tabz, reduced(place[2:3]))):
        c, s = harmonics(fraction, 0)
        cu, su = upper(c, s)
        target[24:32, lanes] = jnp.zeros_like(c)
        target[0:8, lanes] = c
        target[8:13, lanes] = cu[0:5]
        target[13:20, lanes] = s[1:8]
        target[20:25, lanes] = su[0:5]


def partial_kernel(bead_ref, contraction_hbm, coords_hbm, keep_ref, send_ref, contraction_ref, coords_ref, sems):
    copies = (
        pltpu.make_async_copy(contraction_hbm, contraction_ref, sems.at[0]),
        pltpu.make_async_copy(coords_hbm, coords_ref, sems.at[1]),
    )
    for copy in copies:
        copy.start()
    bead = bead_ref[0]
    core = bead % 2
    first = 2 * bead
    keep_ref[...] = jnp.zeros_like(keep_ref)
    send_ref[...] = jnp.zeros_like(send_ref)
    for copy in copies:
        copy.wait()
    for c in range(3):
        x0, x1 = coords_ref[c, 0:1, :], coords_ref[c, 1:2, :]
        keep_ref[c : c + 1, :] = contraction_ref[core, first] * x0 + contraction_ref[core, first + 1] * x1
        send_ref[c : c + 1, :] = (
            contraction_ref[1 - core, first] * x0 + contraction_ref[1 - core, first + 1] * x1
        )
        send_ref[3 + c : 4 + c, :] = jnp.where(core == 0, x0, x1)
        send_ref[8 + c : 9 + c, :] = jnp.where(core == 0, x1, x0)


WROWS = (KTOP + 1) * XROWS


def histogram_kernel(wave_ref, out_ref, acc_ref):
    step = 1024
    count = wave_ref.shape[1]
    acc_ref[...] = jnp.zeros_like(acc_ref)
    row = row_iota(16, step)
    wanted = jnp.where(row < 12, row + 1, jnp.where(row == 12, 0, -1))

    def body(index, carry):
        lanes = pl.ds(pl.multiple_of(index * step, step), step)
        h, k, l = wave_ref[0:1, lanes], wave_ref[1:2, lanes], wave_ref[2:3, lanes]
        flip = jnp.where(h < 0, -1, 1)
        h, k, l = h * flip, k * flip, l * flip
        s2 = jnp.where(k < 0, -1.0, 1.0)
        s3 = jnp.where(l < 0, -1.0, 1.0)
        k, l = jnp.abs(k), jnp.abs(l)
        hit = h == wanted
        left = [jnp.where(hit, sign, 0.0) for sign in (jnp.ones_like(s2), s2, s3, s2 * s3)]
        ones = jnp.where(l == row, 1.0, 0.0)
        right = [jnp.where(k == order, ones, 0.0) for order in range(KTOP + 1)]
        acc_ref[:, 0 : 16 * (KTOP + 1)] += lax.dot_general(
            jnp.concatenate(left, 0).astype(jnp.bfloat16),
            jnp.concatenate(right, 0).astype(jnp.bfloat16),
            (((1,), (1,)), ((), ())),
            preferred_element_type=jnp.float32,
        )
        return carry

    lax.fori_loop(0, count // step, body, 0)
    lane = row_iota(8, 128, 1)
    line = row_iota(8, 128)
    kl = TWO_PI * jnp.where(lane <= KTOP, lane, lane - KTOP).astype(jnp.float32)
    side = jnp.where(lane <= KTOP, 1.0, -1.0)
    side = jnp.where(lane == 0, 0.0, side)
    near = (TWO_PI / 16.0) * (line + 1).astype(jnp.float32)
    late = (TWO_PI / 16.0) * ((line & 3) + 9).astype(jnp.float32)
    half = jnp.where(line < 4, 1.0, -1.0)
    out_ref[4 * WROWS :, :] = jnp.zeros((64, 128), jnp.float32)

    def weigh(kh, order):
        ksq = (kh * kh + (TWO_PI * order) ** 2) + kl * kl
        safe = jnp.where(ksq > 0.0, ksq, 1.0)
        weight = (-2.0 * 4.0 * math.pi / 16.0) * jnp.exp(-safe / (4.0 * alpha_split * alpha_split)) / safe
        return jnp.where((lane < SPAN) & (ksq > 0.0), weight, 0.0)

    for order in range(KTOP + 1):
        tile = slice(128 * (order // 8), 128 * (order // 8) + 128)
        at = 16 * (order % 8)
        first, second, zero = weigh(near, order), weigh(late, order), weigh(jnp.zeros_like(near), order)
        for moment in range(4):
            found = []
            for part in range(2):
                counts = acc_ref[16 * moment + 8 * part : 16 * moment + 8 * part + 8, tile]
                low = pltpu.roll(counts, 128 - at, 1) if at else counts
                both = jnp.where(lane <= KTOP, low, pltpu.roll(low, KTOP, 1))
                found.append(both * side if moment >= 2 else both)
            base = moment * WROWS + order * XROWS
            top = found[0] * first
            middle = jnp.where(line < 4, found[1], pltpu.roll(found[1], 4, 0)) * second
            flipped = moment in (1, 2)
            out_ref[base : base + 8, :] = top
            out_ref[base + 8 : base + 16, :] = middle * half if flipped else middle
            out_ref[base + 16 : base + 24, :] = -top if flipped else top
            if moment in (0, 3):
                plain = (found[1] * zero)[4:5]
                start = 4 * WROWS + (32 if moment else 0)
                if order or not moment:
                    out_ref[start + order : start + order + 1, :] = -plain if moment else plain
                if order:
                    out_ref[start + KTOP + order : start + KTOP + order + 1, :] = plain


def factor_kernel(
    counts_ref, near_ref, far_ref, charge_ref, out_ref, tabx, taby, tabz, right, total_ref
):
    slots = near_ref.shape[1]
    right[64:128, :] = jnp.zeros((64, STEP), jnp.bfloat16)
    total_ref[...] = jnp.zeros_like(total_ref)

    def body(index, carry):
        lanes = pl.ds(pl.multiple_of(index * STEP, STEP), STEP)
        place = near_ref[0:3, lanes] + far_ref[0:3, lanes]
        live = row_iota(1, STEP, 1) + index * STEP < counts_ref[0]
        charge = jnp.where(live, charge_ref[0:1, lanes], 0.0)
        tables(place, tabx, taby, tabz, lanes)
        high, low = split(tabz[:, lanes] * charge)
        right[0:32, :] = high
        right[32:64, :] = low
        other = right[...]
        dims = (((1,), (1,)), ((), ()))
        column = tabx[:, lanes]
        for group in range(GROUPS):
            blocks = [column * taby[5 * group + j : 5 * group + j + 1, lanes] for j in range(5)]
            blocks.append(taby[5 * group : 5 * group + 8, lanes])
            high, low = split(jnp.concatenate(blocks, 0))
            rows = slice(128 * group, 128 * group + 128)
            total_ref[rows, :] += lax.dot_general(
                high, other, dims, preferred_element_type=jnp.float32
            ) + lax.dot_general(low, other, dims, preferred_element_type=jnp.float32)
        return carry

    lax.fori_loop(0, slots // STEP, body, 0)
    lane128 = row_iota(128, 128, 1)
    packed = jnp.zeros((128, 128), jnp.float32)
    for group in range(GROUPS):
        part = total_ref[128 * group : 128 * group + 128, :]
        part = part + pltpu.roll(part, 96, 1)
        part = jnp.where(lane128 < SPAN, part, 0.0)
        packed = packed + (pltpu.roll(part, SPAN * group, 1) if group else part)
    out_ref[...] = packed


def spread(value):
    high = value.astype(jnp.bfloat16).astype(jnp.float32)
    low = value - high
    return (high + pltpu.roll(high, 32, 1)) + (pltpu.roll(low, 64, 1) + pltpu.roll(low, 96, 1))


def other_z(value):
    lane = row_iota(value.shape[0], 128, 1)
    return jnp.where(lane <= KTOP, pltpu.roll(value, 128 - KTOP, 1), pltpu.roll(value, KTOP, 1))


def other_x(value):
    return jnp.concatenate([value[16:24], pltpu.roll(value[8:16], 4, 0), value[0:8]], 0)


def mix(sums, w_ref, mixed, unpacked, zero_ref, swap_ref):
    zero_ref[...] = jnp.zeros_like(zero_ref)
    swap_ref[...] = jnp.zeros_like(swap_ref)
    total = (sums[0][...] + sums[1][...]) + (sums[2][...] + sums[3][...])
    for group in range(GROUPS):
        rolled = pltpu.roll(total, 128 - SPAN * group, 1) if group else total
        unpacked[128 * group : 128 * group + 128, :] = rolled
        zero_ref[5 * group : 5 * group + 5, :] = rolled[120:125]

    def rows(b):
        start = 128 * (b // 5) + XROWS * (b % 5)
        return slice(start, start + XROWS)

    for order in range(KTOP + 1):
        w0, w2, w3, w23 = [
            w_ref[m * WROWS + order * XROWS : m * WROWS + (order + 1) * XROWS, :] for m in range(4)
        ]
        even = unpacked[rows(order), :]
        even_z = other_z(even)
        if order == 0:
            unpacked[rows(0), :] = spread(w0 * even - w3 * other_x(even_z))
            continue
        odd = unpacked[rows(KTOP + order), :]
        odd_z = other_z(odd)
        first = (w0 * even - w2 * other_x(odd)) - (w3 * other_x(even_z) + w23 * odd_z)
        second = (w0 * odd + w2 * other_x(even)) - (w3 * other_x(odd_z) - w23 * even_z)
        unpacked[rows(order), :] = spread(first)
        unpacked[rows(KTOP + order), :] = spread(second)
    swap_ref[1:13, :] = zero_ref[13:25, :]
    swap_ref[13:25, :] = zero_ref[1:13, :]
    base = 4 * WROWS
    value = w_ref[base : base + 32, :] * zero_ref[...] + w_ref[base + 32 : base + 64, :] * other_z(swap_ref[...])
    zero_ref[...] = spread(value)
    line = row_iota(8, 128)
    for group in range(GROUPS):
        part = zero_ref[5 * group : 5 * group + 8, :]
        unpacked[128 * group + 120 : 128 * group + 128, :] = jnp.where(line < 5, part, 0.0)
    mixed[...] = unpacked[...].astype(jnp.bfloat16)


def force_kernel(
    counts_ref, charge_ref, tabx, taby, tabz, s0_ref, s1_ref, s2_ref, s3_ref, w_ref,
    out_ref, basis, slope, mixed, unpacked, zero_ref, swap_ref, flat, tilt, steep,
):
    slots = charge_ref.shape[1]
    mix((s0_ref, s1_ref, s2_ref, s3_ref), w_ref, mixed, unpacked, zero_ref, swap_ref)
    line = row_iota(32, STEP)
    order_z = TWO_PI * jnp.where(line <= KTOP, line, line - KTOP).astype(jnp.float32)
    order_12 = TWO_PI * (row_iota(12, STEP) + 1).astype(jnp.float32)
    line = row_iota(8, STEP)
    near = (TWO_PI / 16.0) * (line + 1).astype(jnp.float32)
    late = (TWO_PI / 16.0) * ((line & 3) + 9).astype(jnp.float32)
    late = jnp.where(line < 4, -late, late)
    steep[...] = jnp.zeros_like(steep)

    def body(index, carry):
        lanes = pl.ds(pl.multiple_of(index * STEP, STEP), STEP)
        live = row_iota(1, STEP, 1) + index * STEP < counts_ref[0]
        charge = jnp.where(live, charge_ref[0:1, lanes], 0.0)
        z = tabz[:, lanes]
        steep[1:13, :] = -order_12 * tabz[13:25, lanes]
        steep[13:25, :] = order_12 * tabz[1:13, lanes]
        for target, value in ((basis, z), (slope, steep[...])):
            high, low = split(value)
            target[0:32, :] = high
            target[32:64, :] = low
            target[64:96, :] = high
            target[96:128, :] = low
        flat[...] = jnp.dot(mixed[...], basis[...], preferred_element_type=jnp.float32)
        tilt[...] = jnp.dot(mixed[...], slope[...], preferred_element_type=jnp.float32)
        steep[1:13, :] = -order_12 * taby[13:25, lanes]
        steep[13:25, :] = order_12 * taby[1:13, lanes]
        one = two = three = jnp.zeros((XROWS, STEP), jnp.float32)
        for b in range(SPAN):
            start = 128 * (b // 5) + XROWS * (b % 5)
            rows = slice(start, start + XROWS)
            value = taby[b : b + 1, lanes]
            one = one + value * flat[rows, :]
            three = three + value * tilt[rows, :]
            if b:
                two = two + steep[b : b + 1, :] * flat[rows, :]
        fy = fz = jnp.zeros((8, STEP), jnp.float32)
        for group in range(GROUPS):
            rows = slice(128 * group + 120, 128 * group + 128)
            fy = fy + steep[5 * group : 5 * group + 8, :] * flat[rows, :]
            fz = fz + taby[5 * group : 5 * group + 8, lanes] * tilt[rows, :]
        c, m, s = tabx[0:8, lanes], tabx[8:16, lanes], tabx[16:24, lanes]
        fx = near * (c * one[16:24] - s * one[0:8]) + late * (pltpu.roll(m, 4, 0) * one[8:16])
        fy = fy + (c * two[0:8] + m * two[8:16]) + s * two[16:24]
        fz = fz + (c * three[0:8] + m * three[8:16]) + s * three[16:24]
        for row, value in enumerate((fx, fy, fz)):
            out_ref[row : row + 1, lanes] = jnp.sum(value, 0, keepdims=True) * charge
        return carry

    lax.fori_loop(0, slots // STEP, body, 0)


def output_kernel(
    bead_ref, counts_ref, contraction_ref, own_ref, other_ref, coords_ref, inner_ref, far_ref, stiff_ref, out_ref
):
    bead = bead_ref[0]
    core = bead % 2
    first = 2 * bead
    stiff = stiff_ref[...]
    live = row_iota(1, stiff.shape[1], 1) < counts_ref[0]
    for c in range(3):
        own, other = own_ref[c : c + 1, :], other_ref[c : c + 1, :]
        x0, x1 = coords_ref[c, 0:1, :], coords_ref[c, 1:2, :]
        inner, outer = inner_ref[8 + c : 9 + c, :], far_ref[3 + c : 4 + c, :]
        low = jnp.where(core == 0, outer, inner)
        high = jnp.where(core == 0, inner, outer)
        for index, (before, here, after) in enumerate(((low, x0, x1), (x0, x1, high))):
            spring = stiff * ((after + before) - 2.0 * here)
            mine = contraction_ref[core, first + index] * own
            value = (mine + contraction_ref[1 - core, first + index] * other) + spring
            out_ref[c, index : index + 1, :] = jnp.where(live, value, 0.0)


def vmem():
    return pl.BlockSpec(memory_space=pltpu.VMEM)


def smem():
    return pl.BlockSpec(memory_space=pltpu.SMEM)


def hbm():
    return pl.BlockSpec(memory_space=pltpu.HBM)


def call(kernel, shapes, scalars, arrays, scratch, name, flops, limit=16 << 20, specs=None):
    outs = [jax.ShapeDtypeStruct(shape, jnp.float32) for shape in shapes]
    result = pl.pallas_call(
        kernel,
        out_shape=outs,
        in_specs=[smem()] * len(scalars) + (specs or [vmem()] * len(arrays)),
        out_specs=[vmem()] * len(outs),
        scratch_shapes=scratch,
        name=name,
        compiler_params=pltpu.CompilerParams(vmem_limit_bytes=limit),
        cost_estimate=pl.CostEstimate(flops=flops, bytes_accessed=1 << 18, transcendentals=0),
    )(*scalars, *arrays)
    return result if len(outs) > 1 else result[0]


def call_partial(bead, contraction, coords):
    slots = coords.shape[2]
    scratch = [
        pltpu.SMEM(contraction.shape, jnp.float32),
        pltpu.VMEM(coords.shape, jnp.float32),
        pltpu.SemaphoreType.DMA((2,)),
    ]
    return call(
        partial_kernel, [(8, slots), (16, slots)], (bead,), (contraction, coords), scratch, "partial", 1 << 16,
        specs=[hbm(), hbm()],
    )


def call_histogram(wavevectors):
    scratch = [pltpu.VMEM((64, 256), jnp.float32)]
    return call(histogram_kernel, [(4 * WROWS + 64, 128)], (), (wavevectors,), scratch, "histogram", 1 << 32)


def call_factor(counts, near, far, charge):
    slots = near.shape[1]
    scratch = [pltpu.VMEM((128, STEP), jnp.bfloat16), pltpu.VMEM((128 * GROUPS, 128), jnp.float32)]
    shapes = [(128, 128), (XROWS, slots), (32, slots), (32, slots)]
    return call(factor_kernel, shapes, (counts,), (near, far, charge), scratch, "factor", 1 << 32)


def call_force(counts, charge, tables, sums, weights):
    scratch = [
        pltpu.VMEM((128, STEP), jnp.bfloat16),
        pltpu.VMEM((128, STEP), jnp.bfloat16),
        pltpu.VMEM((128 * GROUPS, 128), jnp.bfloat16),
        pltpu.VMEM((128 * GROUPS, 128), jnp.float32),
        pltpu.VMEM((32, 128), jnp.float32),
        pltpu.VMEM((32, 128), jnp.float32),
        pltpu.VMEM((128 * GROUPS, STEP), jnp.float32),
        pltpu.VMEM((128 * GROUPS, STEP), jnp.float32),
        pltpu.VMEM((32, STEP), jnp.float32),
    ]
    arrays = (charge, *tables, *sums, weights)
    return call(force_kernel, [(3, charge.shape[1])], (counts,), arrays, scratch, "force", 1 << 32)


def call_output(bead, counts, contraction, own, other, coords, inner, far, stiffness):
    arrays = (own, other, coords, inner, far, stiffness)
    return call(
        output_kernel, [coords.shape], (bead, counts, contraction), arrays, [], "output", 1 << 16
    )


def shards(mesh_shape, coords, charges, stiffness, counts, contraction, wavevectors):
    beads, bulks = mesh_shape["bead"], mesh_shape["bulk"]
    ys, xs, zs = beads // 4, 4, 2 * (bulks // 4)
    index = lax.axis_index("bead").astype(jnp.int32)
    bead = index.reshape(1)
    core, z_hi = index % 2, index // 2 % 2

    def over_bead(value, target):
        return lax.ppermute(value, "bead", [(i, target(i)) for i in range(beads)])

    def over_x(value, distance):
        pairs = [(i, i // xs * xs + (i + distance) % xs) for i in range(bulks)]
        return lax.ppermute(value, "bulk", pairs)

    def over_z(value, distance):
        pairs = []
        for b in range(beads):
            for k in range(bulks):
                z = (b // 2 % 2) * (zs // 2) + k // xs
                z = (z + distance) % zs
                there = b - b // 2 % 2 * 2 + z // (zs // 2) * 2
                pairs.append((b * bulks + k, there * bulks + z % (zs // 2) * xs + k % xs))
        return lax.ppermute(value, ("bead", "bulk"), pairs)

    charge = charges.reshape(1, -1)
    stiff = stiffness.reshape(1, -1)
    coords = coords.transpose(1, 0, 2)
    weights = call_histogram(wavevectors)
    keep, send = call_partial(bead, contraction, coords)
    inner = over_bead(send, lambda i: i ^ 1)
    chip = keep + inner[0:8]
    before, after, across = [
        over_bead(chip, lambda i, d=d: (i + 4 * d) % (4 * ys)) for d in (1, ys - 1, 2)
    ]
    passing = jnp.where(core == 0, jnp.where(z_hi == 1, before, chip), jnp.where(z_hi == 0, after, chip))
    positions = lax.broadcasted_iota(jnp.int32, chip.shape, 0) < 3
    near = jnp.where(positions, (chip + before) + (after + across), passing)
    far = over_bead(near, lambda i: i ^ 2)
    sums, *tables = call_factor(counts, near, far, charge)
    moved = [over_x(sums, d) for d in (1, 3, 2)]
    sums = (sums + moved[0]) + (moved[1] + moved[2])
    parts = [sums] + [over_z(sums, d) for d in (1, zs - 1, 2)]
    force = call_force(counts, charge, tables, parts, weights)
    other = over_bead(force, lambda i: i ^ 1)
    result = call_output(bead, counts, contraction, force, other, coords, inner, far, stiff)
    return result.transpose(1, 0, 2)


def solution(mesh):
    shape = dict(mesh.shape)
    return jax.shard_map(
        lambda *arrays: shards(shape, *arrays),
        mesh=mesh,
        in_specs=(P("bead", None, "bulk"), P("bulk"), P("bulk"), P("bulk"), P(), P()),
        out_specs=P("bead", None, "bulk"),
        check_vma=False,
    )
```

```python
import math

import jax
import jax.numpy as jnp
import numpy as np
from jax import lax
from jax.experimental import pallas as pl
from jax.experimental.pallas import tpu as pltpu
from jax.sharding import PartitionSpec as P

alpha_split = 30.0
KTOP = 12
SPAN = 2 * KTOP + 1
XROWS = 2 * KTOP
GROUPS = 5
FACTOR_STEP, FACTOR_UNROLL = 512, 4
FORCE_STEP, FORCE_UNROLL = 256, 8
TWO_PI = 2.0 * math.pi


def fitted(function, count):
    nodes = 0.125 + 0.125 * np.cos(np.pi * (np.arange(64) + 0.5) / 64)
    basis = np.polynomial.chebyshev.Chebyshev.fit(nodes, function(np.sqrt(nodes)), count - 1, domain=[0, 0.25])
    return [float(value) for value in basis.convert(kind=np.polynomial.Polynomial).coef]


COS_FIT = fitted(lambda u: np.cos(2 * np.pi * u), 9)
SIN_FIT = fitted(lambda u: np.sin(2 * np.pi * u) / u, 8)


def horner(coefficients, w):
    value = jnp.full_like(w, coefficients[-1])
    for coefficient in coefficients[-2::-1]:
        value = value * w + coefficient
    return value


def turn(cycles):
    u = cycles - jnp.round(cycles)
    w = u * u
    return horner(COS_FIT, w), u * horner(SIN_FIT, w)


def row_iota(rows, lanes, dim=0):
    return lax.broadcasted_iota(jnp.int32, (rows, lanes), dim)


def harmonics(fraction, start):
    order = (row_iota(8, fraction.shape[1]) + start).astype(jnp.float32)
    return turn(order * fraction)


def upper(c, s):
    c4, s4 = c[4:5], s[4:5]
    c8, s8 = c4 * c4 - s4 * s4, 2.0 * s4 * c4
    return c8 * c - s8 * s, s8 * c + c8 * s


def reduced(value):
    return value - jnp.round(value)


def split(value):
    high = value.astype(jnp.bfloat16)
    low = (value - high.astype(jnp.float32)).astype(jnp.bfloat16)
    return high, low


def tables(place, tabx, taby, tabz, lanes):
    x = reduced(place[0:1] * (1.0 / 16.0))
    order = row_iota(8, x.shape[1]).astype(jnp.float32)
    c, s = turn((order + 1.0) * x)
    c8, s8 = c[7:8], s[7:8]
    early = row_iota(8, x.shape[1]) < 4
    low_c = jnp.where(early, c, pltpu.roll(c, 4, 0))
    low_s = jnp.where(early, s, pltpu.roll(s, 4, 0))
    tabx[0:8, lanes] = c
    tabx[8:16, lanes] = jnp.where(early, c8 * low_c - s8 * low_s, s8 * low_c + c8 * low_s)
    tabx[16:24, lanes] = s
    for target, fraction in ((taby, reduced(place[1:2])), (tabz, reduced(place[2:3]))):
        c, s = harmonics(fraction, 0)
        cu, su = upper(c, s)
        target[24:32, lanes] = jnp.zeros_like(c)
        target[0:8, lanes] = c
        target[8:13, lanes] = cu[0:5]
        target[13:20, lanes] = s[1:8]
        target[20:25, lanes] = su[0:5]


def partial_kernel(bead_ref, contraction_hbm, coords_hbm, keep_ref, send_ref, contraction_ref, coords_ref, sems):
    copies = (
        pltpu.make_async_copy(contraction_hbm, contraction_ref, sems.at[0]),
        pltpu.make_async_copy(coords_hbm, coords_ref, sems.at[1]),
    )
    for copy in copies:
        copy.start()
    bead = bead_ref[0]
    core = bead % 2
    first = 2 * bead
    keep_ref[...] = jnp.zeros_like(keep_ref)
    send_ref[...] = jnp.zeros_like(send_ref)
    for copy in copies:
        copy.wait()
    for c in range(3):
        x0, x1 = coords_ref[c, 0:1, :], coords_ref[c, 1:2, :]
        keep_ref[c : c + 1, :] = contraction_ref[core, first] * x0 + contraction_ref[core, first + 1] * x1
        send_ref[c : c + 1, :] = (
            contraction_ref[1 - core, first] * x0 + contraction_ref[1 - core, first + 1] * x1
        )
        send_ref[3 + c : 4 + c, :] = jnp.where(core == 0, x0, x1)
        send_ref[8 + c : 9 + c, :] = jnp.where(core == 0, x1, x0)


WROWS = (KTOP + 1) * XROWS


def histogram_kernel(wave_ref, out_ref, acc_ref):
    step = 1024
    count = wave_ref.shape[1]
    acc_ref[...] = jnp.zeros_like(acc_ref)
    row = row_iota(16, step)
    wanted = jnp.where(row < 12, row + 1, jnp.where(row == 12, 0, -1))

    def body(index, carry):
        lanes = pl.ds(pl.multiple_of(index * step, step), step)
        h, k, l = wave_ref[0:1, lanes], wave_ref[1:2, lanes], wave_ref[2:3, lanes]
        flip = jnp.where(h < 0, -1, 1)
        h, k, l = h * flip, k * flip, l * flip
        s2 = jnp.where(k < 0, -1.0, 1.0)
        s3 = jnp.where(l < 0, -1.0, 1.0)
        k, l = jnp.abs(k), jnp.abs(l)
        hit = h == wanted
        left = [jnp.where(hit, sign, 0.0) for sign in (jnp.ones_like(s2), s2, s3, s2 * s3)]
        ones = jnp.where(l == row, 1.0, 0.0)
        right = [jnp.where(k == order, ones, 0.0) for order in range(KTOP + 1)]
        acc_ref[:, 0 : 16 * (KTOP + 1)] += lax.dot_general(
            jnp.concatenate(left, 0).astype(jnp.bfloat16),
            jnp.concatenate(right, 0).astype(jnp.bfloat16),
            (((1,), (1,)), ((), ())),
            preferred_element_type=jnp.float32,
        )
        return carry

    lax.fori_loop(0, count // step, body, 0)
    lane = row_iota(8, 128, 1)
    line = row_iota(8, 128)
    kl = TWO_PI * jnp.where(lane <= KTOP, lane, lane - KTOP).astype(jnp.float32)
    side = jnp.where(lane <= KTOP, 1.0, -1.0)
    side = jnp.where(lane == 0, 0.0, side)
    near = (TWO_PI / 16.0) * (line + 1).astype(jnp.float32)
    late = (TWO_PI / 16.0) * ((line & 3) + 9).astype(jnp.float32)
    half = jnp.where(line < 4, 1.0, -1.0)
    out_ref[4 * WROWS :, :] = jnp.zeros((64, 128), jnp.float32)

    def weigh(kh, order):
        ksq = (kh * kh + (TWO_PI * order) ** 2) + kl * kl
        safe = jnp.where(ksq > 0.0, ksq, 1.0)
        weight = (-2.0 * 4.0 * math.pi / 16.0) * jnp.exp(-safe / (4.0 * alpha_split * alpha_split)) / safe
        return jnp.where((lane < SPAN) & (ksq > 0.0), weight, 0.0)

    for order in range(KTOP + 1):
        tile = slice(128 * (order // 8), 128 * (order // 8) + 128)
        at = 16 * (order % 8)
        first, second, zero = weigh(near, order), weigh(late, order), weigh(jnp.zeros_like(near), order)
        for moment in range(4):
            found = []
            for part in range(2):
                counts = acc_ref[16 * moment + 8 * part : 16 * moment + 8 * part + 8, tile]
                low = pltpu.roll(counts, 128 - at, 1) if at else counts
                both = jnp.where(lane <= KTOP, low, pltpu.roll(low, KTOP, 1))
                found.append(both * side if moment >= 2 else both)
            base = moment * WROWS + order * XROWS
            top = found[0] * first
            middle = jnp.where(line < 4, found[1], pltpu.roll(found[1], 4, 0)) * second
            flipped = moment in (1, 2)
            out_ref[base : base + 8, :] = top
            out_ref[base + 8 : base + 16, :] = middle * half if flipped else middle
            out_ref[base + 16 : base + 24, :] = -top if flipped else top
            if moment in (0, 3):
                plain = (found[1] * zero)[4:5]
                start = 4 * WROWS + (32 if moment else 0)
                if order or not moment:
                    out_ref[start + order : start + order + 1, :] = -plain if moment else plain
                if order:
                    out_ref[start + KTOP + order : start + KTOP + order + 1, :] = plain


def in_chunks(slots, step, unroll, chunk):
    wide = step * unroll

    def body(index, carry):
        for inner in range(unroll):
            chunk(pl.multiple_of(index * wide + inner * step, step), inner)
        return carry

    if wide == slots:
        for inner in range(unroll):
            chunk(inner * step, inner)
    else:
        lax.fori_loop(0, slots // wide, body, 0)


def factor_kernel(counts_ref, near_ref, far_ref, charge_ref, out_ref, tabx, taby, tabz, total_ref):
    slots = near_ref.shape[1]
    total_ref[...] = jnp.zeros_like(total_ref)
    padding = jnp.zeros((64, FACTOR_STEP), jnp.bfloat16)

    def chunk(start, slot):
        lanes = pl.ds(start, FACTOR_STEP)
        place = near_ref[0:3, lanes] + far_ref[0:3, lanes]
        live = row_iota(1, FACTOR_STEP, 1) + start < counts_ref[0]
        charge = jnp.where(live, charge_ref[0:1, lanes], 0.0)
        tables(place, tabx, taby, tabz, lanes)
        high, low = split(tabz[:, lanes] * charge)
        other = jnp.concatenate([high, low, padding], 0)
        dims = (((1,), (1,)), ((), ()))
        column = tabx[:, lanes]
        for group in range(GROUPS):
            blocks = [column * taby[5 * group + j : 5 * group + j + 1, lanes] for j in range(5)]
            blocks.append(taby[5 * group : 5 * group + 8, lanes])
            high, low = split(jnp.concatenate(blocks, 0))
            rows = slice(128 * group, 128 * group + 128)
            total_ref[rows, :] += lax.dot_general(
                high, other, dims, preferred_element_type=jnp.float32
            ) + lax.dot_general(low, other, dims, preferred_element_type=jnp.float32)

    in_chunks(slots, FACTOR_STEP, FACTOR_UNROLL, chunk)
    lane128 = row_iota(128, 128, 1)
    packed = jnp.zeros((128, 128), jnp.float32)
    for group in range(GROUPS):
        part = total_ref[128 * group : 128 * group + 128, :]
        part = part + pltpu.roll(part, 96, 1)
        part = jnp.where(lane128 < SPAN, part, 0.0)
        packed = packed + (pltpu.roll(part, SPAN * group, 1) if group else part)
    out_ref[...] = packed


def spread(value):
    value = value + pltpu.roll(value, 32, 1)
    value = value + pltpu.roll(value, 64, 1)
    high = value.astype(jnp.bfloat16).astype(jnp.float32)
    return jnp.where(row_iota(value.shape[0], 128, 1) < 64, high, value - high)


def other_z(value):
    lane = row_iota(value.shape[0], 128, 1)
    return jnp.where(lane <= KTOP, pltpu.roll(value, 128 - KTOP, 1), pltpu.roll(value, KTOP, 1))


def other_x(value):
    return jnp.concatenate([value[16:24], pltpu.roll(value[8:16], 4, 0), value[0:8]], 0)


def mix(sums, w_ref, mixed, unpacked, zero_ref, swap_ref):
    zero_ref[...] = jnp.zeros_like(zero_ref)
    swap_ref[...] = jnp.zeros_like(swap_ref)
    total = (sums[0][...] + sums[1][...]) + (sums[2][...] + sums[3][...])
    for group in range(GROUPS):
        rolled = pltpu.roll(total, 128 - SPAN * group, 1) if group else total
        unpacked[128 * group : 128 * group + 128, :] = rolled
        zero_ref[5 * group : 5 * group + 5, :] = rolled[120:125]

    def rows(b):
        start = 128 * (b // 5) + XROWS * (b % 5)
        return slice(start, start + XROWS)

    for order in range(KTOP + 1):
        w0, w2, w3, w23 = [
            w_ref[m * WROWS + order * XROWS : m * WROWS + (order + 1) * XROWS, :] for m in range(4)
        ]
        even = unpacked[rows(order), :]
        even_z = other_z(even)
        if order == 0:
            unpacked[rows(0), :] = spread(w0 * even - w3 * other_x(even_z))
            continue
        odd = unpacked[rows(KTOP + order), :]
        odd_z = other_z(odd)
        first = (w0 * even - w2 * other_x(odd)) - (w3 * other_x(even_z) + w23 * odd_z)
        second = (w0 * odd + w2 * other_x(even)) - (w3 * other_x(odd_z) - w23 * even_z)
        unpacked[rows(order), :] = spread(first)
        unpacked[rows(KTOP + order), :] = spread(second)
    swap_ref[1:13, :] = zero_ref[13:25, :]
    swap_ref[13:25, :] = zero_ref[1:13, :]
    base = 4 * WROWS
    value = w_ref[base : base + 32, :] * zero_ref[...] + w_ref[base + 32 : base + 64, :] * other_z(swap_ref[...])
    zero_ref[...] = spread(value)
    line = row_iota(8, 128)
    for group in range(GROUPS):
        part = zero_ref[5 * group : 5 * group + 8, :]
        unpacked[128 * group + 120 : 128 * group + 128, :] = jnp.where(line < 5, part, 0.0)
    mixed[...] = unpacked[...].astype(jnp.bfloat16)


def force_kernel(
    counts_ref, charge_ref, tabx, taby, tabz, s0_ref, s1_ref, s2_ref, s3_ref, w_ref, unused_ref,
    out_ref, mixed, unpacked, zero_ref, swap_ref, flat_refs, tilt_refs, steep_refs,
):
    slots = charge_ref.shape[1]
    step = FORCE_STEP
    mix((s0_ref, s1_ref, s2_ref, s3_ref), w_ref, mixed, unpacked, zero_ref, swap_ref)
    order_12 = TWO_PI * (row_iota(12, step) + 1).astype(jnp.float32)
    line = row_iota(8, step)
    near = (TWO_PI / 16.0) * (line + 1).astype(jnp.float32)
    late = (TWO_PI / 16.0) * ((line & 3) + 9).astype(jnp.float32)
    late = jnp.where(line < 4, -late, late)
    steep_refs[...] = jnp.zeros_like(steep_refs)

    def chunk(start, slot):
        flat, tilt = flat_refs.at[slot], tilt_refs.at[slot]
        steep_z, steep = steep_refs.at[2 * slot], steep_refs.at[2 * slot + 1]
        lanes = pl.ds(start, step)
        live = row_iota(1, step, 1) + start < counts_ref[0]
        charge = jnp.where(live, charge_ref[0:1, lanes], 0.0)
        steep_z[1:13, :] = -order_12 * tabz[13:25, lanes]
        steep_z[13:25, :] = order_12 * tabz[1:13, lanes]
        steep[1:13, :] = -order_12 * taby[13:25, lanes]
        steep[13:25, :] = order_12 * taby[1:13, lanes]
        for target, value in ((flat, tabz[:, lanes]), (tilt, steep_z[...])):
            high, low = split(value)
            basis = jnp.concatenate([high, low, high, low], 0)
            target[...] = jnp.dot(mixed[...], basis, preferred_element_type=jnp.float32)
        one = two = three = jnp.zeros((XROWS, step), jnp.float32)
        for b in range(SPAN):
            first = 128 * (b // 5) + XROWS * (b % 5)
            rows = slice(first, first + XROWS)
            value = taby[b : b + 1, lanes]
            one = one + value * flat[rows, :]
            three = three + value * tilt[rows, :]
            if b:
                two = two + steep[b : b + 1, :] * flat[rows, :]
        fy = fz = jnp.zeros((8, step), jnp.float32)
        for group in range(GROUPS):
            rows = slice(128 * group + 120, 128 * group + 128)
            fy = fy + steep[5 * group : 5 * group + 8, :] * flat[rows, :]
            fz = fz + taby[5 * group : 5 * group + 8, lanes] * tilt[rows, :]
        c, m, s = tabx[0:8, lanes], tabx[8:16, lanes], tabx[16:24, lanes]
        fx = near * (c * one[16:24] - s * one[0:8]) + late * (pltpu.roll(m, 4, 0) * one[8:16])
        fy = fy + (c * two[0:8] + m * two[8:16]) + s * two[16:24]
        fz = fz + (c * three[0:8] + m * three[8:16]) + s * three[16:24]
        for row, value in enumerate((fx, fy, fz)):
            out_ref[row : row + 1, lanes] = jnp.sum(value, 0, keepdims=True) * charge

    in_chunks(slots, step, FORCE_UNROLL, chunk)


def spring_kernel(
    bead_ref, counts_ref, contraction_ref, coords_ref, inner_ref, far_ref, stiff_ref, spring_ref, weight_ref
):
    bead = bead_ref[0]
    core = bead % 2
    first = 2 * bead
    live = row_iota(1, stiff_ref.shape[1], 1) < counts_ref[0]
    stiff = jnp.where(live, stiff_ref[...], 0.0)
    for index in range(2):
        for side, replica in enumerate((core, 1 - core)):
            row = 2 * side + index
            weight_ref[row : row + 1, :] = jnp.where(live, contraction_ref[replica, first + index], 0.0)
    for c in range(3):
        x0, x1 = coords_ref[c, 0:1, :], coords_ref[c, 1:2, :]
        inner, outer = inner_ref[8 + c : 9 + c, :], far_ref[3 + c : 4 + c, :]
        low = jnp.where(core == 0, outer, inner)
        high = jnp.where(core == 0, inner, outer)
        spring_ref[c, 0:1, :] = stiff * ((x1 + low) - 2.0 * x0)
        spring_ref[c, 1:2, :] = stiff * ((high + x0) - 2.0 * x1)


def output_kernel(own_ref, other_ref, spring_ref, weight_ref, out_ref):
    for c in range(3):
        own, other = own_ref[c : c + 1, :], other_ref[c : c + 1, :]
        for index in range(2):
            value = weight_ref[index : index + 1, :] * own + weight_ref[2 + index : 3 + index, :] * other
            out_ref[c, index : index + 1, :] = value + spring_ref[c, index : index + 1, :]


def vmem():
    return pl.BlockSpec(memory_space=pltpu.VMEM)


def smem():
    return pl.BlockSpec(memory_space=pltpu.SMEM)


def hbm():
    return pl.BlockSpec(memory_space=pltpu.HBM)


def call(kernel, shapes, scalars, arrays, scratch, name, flops, limit=16 << 20, specs=None):
    outs = [jax.ShapeDtypeStruct(shape, jnp.float32) for shape in shapes]
    result = pl.pallas_call(
        kernel,
        out_shape=outs,
        in_specs=[smem()] * len(scalars) + (specs or [vmem()] * len(arrays)),
        out_specs=[vmem()] * len(outs),
        scratch_shapes=scratch,
        name=name,
        compiler_params=pltpu.CompilerParams(vmem_limit_bytes=limit),
        cost_estimate=pl.CostEstimate(flops=flops, bytes_accessed=1 << 18, transcendentals=0),
    )(*scalars, *arrays)
    return result if len(outs) > 1 else result[0]


def call_partial(bead, contraction, coords):
    slots = coords.shape[2]
    scratch = [
        pltpu.SMEM(contraction.shape, jnp.float32),
        pltpu.VMEM(coords.shape, jnp.float32),
        pltpu.SemaphoreType.DMA((2,)),
    ]
    return call(
        partial_kernel, [(8, slots), (16, slots)], (bead,), (contraction, coords), scratch, "partial", 1 << 16,
        specs=[hbm(), hbm()],
    )


def call_histogram(wavevectors):
    scratch = [pltpu.VMEM((64, 256), jnp.float32)]
    return call(histogram_kernel, [(4 * WROWS + 64, 128)], (), (wavevectors,), scratch, "histogram", 1 << 32)


def call_factor(counts, near, far, charge):
    slots = near.shape[1]
    scratch = [pltpu.VMEM((128 * GROUPS, 128), jnp.float32)]
    shapes = [(128, 128), (XROWS, slots), (32, slots), (32, slots)]
    return call(factor_kernel, shapes, (counts,), (near, far, charge), scratch, "factor", 1 << 32)


def call_force(counts, charge, tables, sums, weights, earlier):
    scratch = [
        pltpu.VMEM((128 * GROUPS, 128), jnp.bfloat16),
        pltpu.VMEM((128 * GROUPS, 128), jnp.float32),
        pltpu.VMEM((32, 128), jnp.float32),
        pltpu.VMEM((32, 128), jnp.float32),
        pltpu.VMEM((FORCE_UNROLL, 128 * GROUPS, FORCE_STEP), jnp.float32),
        pltpu.VMEM((FORCE_UNROLL, 128 * GROUPS, FORCE_STEP), jnp.float32),
        pltpu.VMEM((2 * FORCE_UNROLL, 32, FORCE_STEP), jnp.float32),
    ]
    arrays = (charge, *tables, *sums, weights, earlier)
    return call(force_kernel, [(3, charge.shape[1])], (counts,), arrays, scratch, "force", 1 << 32)


def call_spring(bead, counts, contraction, coords, inner, far, stiffness):
    shapes = [coords.shape, (4, coords.shape[2])]
    arrays = (coords, inner, far, stiffness)
    return call(spring_kernel, shapes, (bead, counts, contraction), arrays, [], "spring", 1 << 30)


def call_output(own, other, spring, weight):
    return call(output_kernel, [spring.shape], (), (own, other, spring, weight), [], "output", 1 << 16)


def shards(mesh_shape, coords, charges, stiffness, counts, contraction, wavevectors):
    beads, bulks = mesh_shape["bead"], mesh_shape["bulk"]
    ys, xs, zs = beads // 4, 4, 2 * (bulks // 4)
    index = lax.axis_index("bead").astype(jnp.int32)
    bead = index.reshape(1)
    core, z_hi = index % 2, index // 2 % 2

    def over_bead(value, target):
        return lax.ppermute(value, "bead", [(i, target(i)) for i in range(beads)])

    def over_x(value, distance):
        pairs = [(i, i // xs * xs + (i + distance) % xs) for i in range(bulks)]
        return lax.ppermute(value, "bulk", pairs)

    def over_z(value, distance):
        pairs = []
        for b in range(beads):
            for k in range(bulks):
                z = (b // 2 % 2) * (zs // 2) + k // xs
                z = (z + distance) % zs
                there = b - b // 2 % 2 * 2 + z // (zs // 2) * 2
                pairs.append((b * bulks + k, there * bulks + z % (zs // 2) * xs + k % xs))
        return lax.ppermute(value, ("bead", "bulk"), pairs)

    charge = charges.reshape(1, -1)
    stiff = stiffness.reshape(1, -1)
    coords = coords.transpose(1, 0, 2)
    weights = call_histogram(wavevectors)
    pinned = [pltpu.with_memory_space_constraint(value, pltpu.HBM) for value in (contraction, coords)]
    keep, send = call_partial(bead, *pinned)
    inner = over_bead(send, lambda i: i ^ 1)
    chip = keep + inner[0:8]
    before, after, across = [
        over_bead(chip, lambda i, d=d: (i + 4 * d) % (4 * ys)) for d in (1, ys - 1, 2)
    ]
    passing = jnp.where(core == 0, jnp.where(z_hi == 1, before, chip), jnp.where(z_hi == 0, after, chip))
    positions = lax.broadcasted_iota(jnp.int32, chip.shape, 0) < 3
    near = jnp.where(positions, (chip + before) + (after + across), passing)
    far = over_bead(near, lambda i: i ^ 2)
    sums, *tables = call_factor(counts, near, far, charge)
    moved = [over_x(sums, d) for d in (1, 3, 2)]
    sums = (sums + moved[0]) + (moved[1] + moved[2])
    parts = [sums] + [over_z(sums, d) for d in (1, zs - 1, 2)]
    spring, shares = call_spring(bead, counts, contraction, coords, inner, far, stiff)
    force = call_force(counts, charge, tables, parts, weights, shares)
    other = over_bead(force, lambda i: i ^ 1)
    result = call_output(force, other, spring, shares)
    return result.transpose(1, 0, 2)


def solution(mesh):
    shape = dict(mesh.shape)
    return jax.shard_map(
        lambda *arrays: shards(shape, *arrays),
        mesh=mesh,
        in_specs=(P("bead", None, "bulk"), P("bulk"), P("bulk"), P("bulk"), P(), P()),
        out_specs=P("bead", None, "bulk"),
        check_vma=False,
    )
```
